32 devices in a mesh: groups: 2 (over y), col: 4 (over z), row: 2 (over x), side: 2 (over core).
Axes of the slice: x: 2, y: 2, z: 4, core: 2. Of those that a mesh axis runs over, the one named last changes fastest.
Arguments:
- hidden_in: bfloat16 [256, 8192], P(('groups', 'col'), 'row'), parts along dimension 0, may hold values from -40 to 40
- norm_gain: bfloat16 [8192], P('row'), may hold values from 0.099609375 to 1.8984375
- qkv_weight: bfloat16 [8192, 10240], P('row', 'col'), may hold values from -0.0625 to 0.0625
- out_weight: bfloat16 [8192, 8192], P('row', 'col'), may hold values from -0.0625 to 0.0625
- key_cache: bfloat16 [256, 64, 1024], P(('groups', 'col'), None, 'row'), parts along dimension 0, may hold values from -320 to 320
- value_cache: bfloat16 [256, 64, 1024], P(('groups', 'col'), None, 'row'), parts along dimension 0, may hold values from -4 to 4
- cache_lengths: int32 [256], P(('groups', 'col')), parts along dimension 0, may hold values from 1 to 64, 4096 in all
- slot_request: int32 [256], P('groups'), parts along dimension 0, may hold values from 0 to 127, each once
Outputs:
- layer_rows: bfloat16 [2, 256, 8192], P('side', ('groups', 'col'), 'row'), parts along dimension 1
The draws below stay inside these ranges and needn't reach their ends.
There are 2 independent parts, one for each index of `groups`. The reference program is written for one: setup_inputs(seed, part) draws one part's arguments, and reference() takes and returns one part's arrays. A program takes and returns all parts, laid end to end along the dimension named above; an argument that names none is the same for every part. Nothing has to cross between parts.
Inputs may be any that keep to these rules, and one draw needn't show every extreme that they name: Slot s of cache_lengths, key_cache and value_cache belongs to request slot_request[s]; every request has exactly one slot. Positions from cache_lengths[s] on are not filled; some slot is full in every draw.
All inputs are finite; a program needn't handle non-finite values. No bound on the sum of `cache_lengths` on one device may be relied on, other than what follows from the above.
Results may differ from the reference program's by a relative error of at most 0.035.
Values may be sent and summed in bfloat16 or wider, within the bound.
A program may use at most 128 MiB of HBM per device.

```python
import math
import jax
import jax.numpy as jnp
import numpy as np
from jax import lax

D = 8192
HEADS = 64
KV_HEADS = 8
HEAD_DIM = 128
CACHE = 64
QKV = 10240
REQUESTS = 128


def draw_hidden_in(key, part):
    noise_key, row_key, col_key = jax.random.split(key, 3)
    columns = jnp.arange(D, dtype=jnp.float32) / D
    noise_vals = jnp.clip(jax.random.normal(noise_key, (REQUESTS, D), jnp.float32), -3.0, 3.0)
    row_scale = jnp.exp(math.log(10.0) * (jax.random.uniform(row_key, (REQUESTS, 1), jnp.float32) - 0.5))
    col_trend = jnp.exp(math.log(3.0) * (columns - 0.5))
    jitter = jnp.exp(math.log(3.0) * (jax.random.uniform(col_key, (1, D), jnp.float32) - 0.5))
    return (noise_vals * row_scale * jitter * col_trend[None, :]).astype(jnp.bfloat16)


def draw_key_cache(key, part):
    noise_key = jax.random.fold_in(key, 0)
    values = jnp.clip(jax.random.normal(noise_key, (REQUESTS, CACHE, KV_HEADS * HEAD_DIM), jnp.float32), -4.0, 4.0)
    return values.astype(jnp.bfloat16)


def levels(own_key, extent, cuts, smallest, largest):
    def one(dim, parts):
        heights = jax.random.uniform(jax.random.fold_in(jax.random.fold_in(own_key, 6), dim), (parts,), jnp.float32, smallest / len(cuts), largest / len(cuts))
        return jnp.repeat(jnp.exp(heights), extent[dim] // parts).reshape((-1,) + (1,) * (len(extent) - dim - 1))

    factor_of = one(*cuts[0])
    for cut in cuts[1:]:
        factor_of = factor_of * one(*cut)
    return factor_of


def length_profile(number_of, total, reach, slope):
    loads = [(1 << 20) // math.isqrt(grade ** slope) + 1 for grade in range(2, number_of + 1)]
    surplus, counts = total - reach - (number_of - 1), [1] * (number_of - 1)
    while surplus > 0:
        free = [i for i in range(number_of - 1) if counts[i] < reach]
        mass, remaining = sum([loads[i] for i in free]), surplus
        for i in free:
            more = min(reach - counts[i], max(1, remaining * loads[i] // mass), surplus)
            counts[i] = counts[i] + more
            surplus = surplus - more
    return np.array([reach] + counts)


def uneven(own_key, number_of, total, reach, skew):
    if number_of == 2:
        one = jax.random.randint(own_key, (), max(1, total - reach), min(reach, total - 1) + 1)
        return jnp.stack([one, total - one])
    sizes = jnp.asarray(length_profile(number_of, total, reach, skew), jnp.int32)
    pairs = (number_of - 1) // 2
    giver, receiver = sizes[1:1 + 2 * pairs:2], sizes[2:2 + 2 * pairs:2]
    slack = jnp.minimum(giver - 1, reach - receiver)
    passed = jax.random.randint(jax.random.fold_in(own_key, 1), (pairs,), 0, 1 << 20) % (slack + 1)
    sizes = sizes.at[1:1 + 2 * pairs:2].set(giver - passed).at[2:2 + 2 * pairs:2].set(receiver + passed)
    return sizes[jax.random.permutation(jax.random.fold_in(own_key, 2), number_of)]


def bell_draw(rng, shape, spread, bound, cuts=(), kind=jnp.bfloat16):
    values = jax.random.normal(rng, shape, jnp.float32) * spread
    if len(cuts) > 0:
        values = levels(rng, shape, cuts, -0.22, 0.18) * values
    return jnp.clip(values, min=-bound, max=bound).astype(kind)


def setup_inputs(seed: int = 0, part: int = 0) -> dict:
    key_list = jax.random.split(jax.random.key(seed), 9)
    part_splits = jax.random.split(jax.random.fold_in(key_list[8], part), 9)
    hidden_in = draw_hidden_in(jax.random.fold_in(jax.random.fold_in(key_list[8], part), 71), part)
    norm_gain = jnp.clip(1.0 + 0.18 * jax.random.normal(key_list[1], (D,), jnp.float32), 0.099609375, 1.8984375).astype(jnp.bfloat16)
    qkv_weight = bell_draw(key_list[2], (D, QKV), D ** -0.5, 0.0625, ((0, 2), (1, 4)))
    out_weight = bell_draw(key_list[3], (D, D), D ** -0.5, 0.0625, ((0, 2), (1, 4)))
    key_cache = draw_key_cache(jax.random.fold_in(jax.random.fold_in(key_list[8], part), 71), part)
    value_cache = bell_draw(part_splits[5], (REQUESTS, CACHE, KV_HEADS * HEAD_DIM), 1.0, 4.0, ((0, 4), (2, 2)))
    cache_lengths = uneven(part_splits[6], REQUESTS, REQUESTS * CACHE // 2, CACHE, 2).astype(jnp.int32)
    slot_request = jax.random.permutation(part_splits[7], REQUESTS).astype(jnp.int32)
    return dict(hidden_in=hidden_in, norm_gain=norm_gain, qkv_weight=qkv_weight, out_weight=out_weight, key_cache=key_cache, value_cache=value_cache, cache_lengths=cache_lengths, slot_request=slot_request)


EPSILON = 1e-05
THETA = 500000.0

def rope_tables(lengths, head_dim):
    half_dim = head_dim // 2
    inv_freq = jnp.exp(-jnp.log(jnp.float32(THETA)) * jnp.arange(half_dim, dtype=jnp.float32) / half_dim)
    phases = lengths.astype(jnp.float32)[:, None] * inv_freq[None, :]
    return (jnp.cos(phases), jnp.sin(phases))

def rotate(vector, cos_vals, sine_vals):
    half_dim = vector.shape[-1] // 2
    front_half = vector[..., :half_dim]
    back_half = vector[..., half_dim:]
    return jnp.concatenate([front_half * cos_vals - back_half * sine_vals, back_half * cos_vals + front_half * sine_vals], axis=-1)

def reference(hidden_in, norm_gain, qkv_weight, out_weight, key_cache, value_cache, cache_lengths, slot_request):
    residual = hidden_in.astype(jnp.float32)
    mean_square = lax.optimization_barrier(jnp.mean(residual * residual, axis=1, keepdims=True))
    normed = (residual * lax.rsqrt(mean_square + EPSILON) * norm_gain.astype(jnp.float32)[None, :]).astype(jnp.bfloat16)
    projected_in = jnp.dot(normed, qkv_weight, preferred_element_type=jnp.float32).astype(jnp.bfloat16)
    slot_count = hidden_in.shape[0]
    per_group = HEADS // KV_HEADS
    grouped = jnp.take(projected_in, slot_request, axis=0).reshape(slot_count, KV_HEADS, per_group + 2, HEAD_DIM)
    cos_vals, sine_vals = rope_tables(cache_lengths, HEAD_DIM)
    queries = rotate(grouped[:, :, :per_group].astype(jnp.float32), cos_vals[:, None, None, :], sine_vals[:, None, None, :]).astype(jnp.bfloat16)
    new_keys = rotate(grouped[:, :, per_group].astype(jnp.float32), cos_vals[:, None, :], sine_vals[:, None, :]).astype(jnp.bfloat16)
    new_values = grouped[:, :, per_group + 1]
    cache_keys = key_cache.reshape(slot_count, CACHE, KV_HEADS, HEAD_DIM).astype(jnp.float32)
    cache_values = value_cache.reshape(slot_count, CACHE, KV_HEADS, HEAD_DIM).astype(jnp.float32)
    factor = HEAD_DIM ** (-0.5)
    cache_scores = jnp.einsum('sghd,slgd->sghl', queries.astype(jnp.float32), cache_keys) * factor
    own_scores = lax.optimization_barrier(jnp.sum(queries.astype(jnp.float32) * new_keys.astype(jnp.float32)[:, :, None, :], axis=-1)) * factor
    in_cache = lax.broadcasted_iota(jnp.int32, (slot_count, CACHE), 1) < cache_lengths[:, None]
    cache_scores = jnp.where(in_cache[:, None, None, :], cache_scores, -1e+30)
    row_max = jnp.maximum(lax.optimization_barrier(jnp.max(cache_scores, axis=-1)), own_scores)
    cache_exp = jnp.exp(cache_scores - row_max[..., None])
    own_exp = jnp.exp(own_scores - row_max)
    denominator = lax.optimization_barrier(jnp.sum(cache_exp, axis=-1)) + own_exp
    cache_weight = (cache_exp / denominator[..., None]).astype(jnp.bfloat16)
    own_weight = (own_exp / denominator).astype(jnp.bfloat16)
    combined = jnp.einsum('sghl,slgd->sghd', cache_weight.astype(jnp.float32), cache_values)
    combined = combined + own_weight.astype(jnp.float32)[..., None] * new_values.astype(jnp.float32)[:, :, None, :]
    attention = combined.astype(jnp.bfloat16).reshape(slot_count, HEADS * HEAD_DIM)
    inverse = jnp.argsort(slot_request).astype(jnp.int32)
    by_request = jnp.take(attention, inverse, axis=0)
    projected = jnp.dot(by_request, out_weight, preferred_element_type=jnp.float32)
    hidden = (residual + projected).astype(jnp.bfloat16)
    return jnp.stack([hidden, attention])
```

```python
import functools

import jax
import jax.numpy as jnp
from jax import lax
from jax.experimental import pallas as pl
from jax.experimental.pallas import tpu as pltpu
from jax.sharding import PartitionSpec as P

D = 8192
HEADS = 64
KV_HEADS = 8
HEAD_DIM = 128
QKV = 10240


EPSILON = 1e-05
THETA = 500000.0


def swapped(value, axis, bit):
    mask = 2**bit
    pairs = [(source, source ^ mask) for source in range(lax.axis_size(axis))]
    return lax.ppermute(value, axis, pairs)


def rope_tables(lengths, head_dim):
    half_dim = head_dim // 2
    inv_freq = jnp.exp(
        -jnp.log(jnp.float32(THETA)) * jnp.arange(half_dim, dtype=jnp.float32) / half_dim
    )
    phases = lengths.astype(jnp.float32)[:, None] * inv_freq[None, :]
    return (jnp.cos(phases), jnp.sin(phases))


def rotate(vector, cos_vals, sine_vals):
    half_dim = vector.shape[-1] // 2
    front_half = vector[..., :half_dim]
    back_half = vector[..., half_dim:]
    return jnp.concatenate(
        [
            front_half * cos_vals - back_half * sine_vals,
            back_half * cos_vals + front_half * sine_vals,
        ],
        axis=-1,
    )


def attend(packed, key_block, value_block, lengths):
    slot_count = packed.shape[0]
    cache_size = key_block.shape[1]
    groups = key_block.shape[2] // HEAD_DIM
    per_group = HEADS // KV_HEADS
    grouped = packed.reshape(slot_count, groups, per_group + 2, HEAD_DIM)
    cos_vals, sine_vals = rope_tables(lengths, HEAD_DIM)
    queries = rotate(
        grouped[:, :, :per_group].astype(jnp.float32),
        cos_vals[:, None, None, :],
        sine_vals[:, None, None, :],
    ).astype(jnp.bfloat16)
    new_keys = rotate(
        grouped[:, :, per_group].astype(jnp.float32), cos_vals[:, None, :], sine_vals[:, None, :]
    ).astype(jnp.bfloat16)
    new_values = grouped[:, :, per_group + 1]
    cache_keys = key_block.reshape(slot_count, cache_size, groups, HEAD_DIM)
    cache_values = value_block.reshape(slot_count, cache_size, groups, HEAD_DIM)
    factor = HEAD_DIM ** (-0.5)
    cache_scores = (
        jnp.einsum("sghd,slgd->sghl", queries, cache_keys, preferred_element_type=jnp.float32)
        * factor
    )
    own_scores = (
        jnp.einsum("sghd,sgd->sgh", queries, new_keys, preferred_element_type=jnp.float32) * factor
    )
    in_cache = lax.broadcasted_iota(jnp.int32, (slot_count, cache_size), 1) < lengths[:, None]
    cache_scores = jnp.where(in_cache[:, None, None, :], cache_scores, -1e30)
    row_max = jnp.maximum(jnp.max(cache_scores, axis=-1), own_scores)
    cache_exp = jnp.exp(cache_scores - row_max[..., None])
    own_exp = jnp.exp(own_scores - row_max)
    denominator = jnp.sum(cache_exp, axis=-1) + own_exp
    cache_weight = (cache_exp / denominator[..., None]).astype(jnp.bfloat16)
    own_weight = (own_exp / denominator).astype(jnp.bfloat16)
    combined = jnp.einsum(
        "sghl,slgd->sghd", cache_weight, cache_values, preferred_element_type=jnp.float32
    )
    combined = (
        combined
        + own_weight.astype(jnp.float32)[..., None] * new_values.astype(jnp.float32)[:, :, None, :]
    )
    return combined.astype(jnp.bfloat16).reshape(slot_count, groups * per_group * HEAD_DIM)


def per_device_general(
    hidden_in,
    norm_gain,
    qkv_weight,
    out_weight,
    key_cache,
    value_cache,
    cache_lengths,
    slot_request,
):
    side_index = lax.axis_index("side")
    is_weight = side_index == 0
    col_count = lax.axis_size("col")
    row_count = lax.axis_size("row")
    group_cols = col_count // row_count
    in_half = qkv_weight.shape[1] // 2
    out_half = out_weight.shape[1] // 2
    residual = hidden_in.astype(jnp.float32)
    square_sums = lax.psum(jnp.sum(residual * residual, axis=1), "row")
    normed = (
        residual
        * lax.rsqrt(square_sums[:, None] / D + EPSILON)
        * norm_gain.astype(jnp.float32)[None, :]
    ).astype(jnp.bfloat16)
    in_weight = lax.dynamic_slice_in_dim(qkv_weight, side_index * in_half, in_half, 1)
    partial_in = jnp.dot(
        lax.all_gather(normed, "col", axis=0, tiled=True),
        in_weight,
        preferred_element_type=jnp.float32,
    )
    in_slots = jnp.take(partial_in, slot_request, axis=0)
    own_width = QKV // row_count
    summed = lax.psum(in_slots.astype(jnp.bfloat16), "row")
    spread = lax.all_to_all(summed, "col", split_axis=0, concat_axis=1, tiled=True)
    own_columns = lax.dynamic_slice_in_dim(
        spread.reshape(spread.shape[0], col_count, in_half),
        lax.axis_index("row") * group_cols,
        group_cols,
        1,
    )
    slot_half = key_cache.shape[0] // 2
    halves = lax.all_to_all(
        own_columns[:, :, None, :], "side", split_axis=0, concat_axis=2, tiled=True
    )
    arrived = halves.reshape(slot_half, own_width)
    first_slot = side_index * slot_half
    key_part = lax.dynamic_slice_in_dim(key_cache, first_slot, slot_half, 0)
    value_part = lax.dynamic_slice_in_dim(value_cache, first_slot, slot_half, 0)
    length_part = lax.dynamic_slice_in_dim(cache_lengths, first_slot, slot_half, 0)
    attended = attend(arrived, key_part, value_part, length_part)
    out_cols = lax.dynamic_slice_in_dim(out_weight, side_index * out_half, out_half, 1)
    collected = lax.all_gather(attended, ("col", "side"), axis=0, tiled=True)
    out_slots = jnp.dot(collected, out_cols, preferred_element_type=jnp.float32)
    inverse = jnp.argsort(slot_request)
    out_requests = jnp.take(out_slots, inverse, axis=0)
    spread_out = lax.all_to_all(
        out_requests.astype(jnp.bfloat16), "col", split_axis=0, concat_axis=1, tiled=True
    ).astype(out_requests.dtype)
    out_view = spread_out.reshape(spread_out.shape[0], col_count, out_half)
    summed_out = lax.psum_scatter(
        out_view.astype(jnp.bfloat16), "row", scatter_dimension=1, tiled=True
    ).astype(jnp.float32)
    req_rows = hidden_in.shape[0]
    residual_view = residual.reshape(req_rows, group_cols, 2, out_half)
    residual_half = lax.dynamic_index_in_dim(residual_view, side_index, 2, keepdims=False)
    own_hidden = (residual_half + summed_out).astype(jnp.bfloat16)
    payload = jnp.where(is_weight, attended, own_hidden.reshape(attended.shape))
    received = swapped(payload, "side", 0)
    hidden = jnp.stack([own_hidden, received.reshape(own_hidden.shape)], axis=2).reshape(
        req_rows, residual.shape[1]
    )
    attention_rows = jnp.concatenate([received, attended], axis=0)
    result = jnp.where(is_weight, hidden, attention_rows)
    return result[None]


MESH = pl.DeviceIdType.MESH
F32 = jnp.float32
BF16 = jnp.bfloat16
TILE = 256


def fused_kernel(
    nz,
    nx,
    hid_any,
    gain_ref,
    wq_any,
    wo_any,
    k_any,
    v_any,
    cos_ref,
    sin_ref,
    len_ref,
    to_slot_ref,
    to_req_ref,
    out_ref,
    wq,
    wo,
    kbuf,
    vbuf,
    hid,
    xg,
    xn,
    sso,
    ssb,
    acc,
    pbuf,
    rbuf,
    fbuf,
    tb,
    af,
    ag,
    yacc,
    ybuf,
    hbuf,
    gbuf,
    load_sem,
    x_recv,
    x_send,
    x_fwd,
    ss_recv,
    ss_send,
    p_recv,
    p_send,
    f_recv,
    f_send,
    a_recv,
    a_send,
    a_fwd,
    y_recv,
    y_send,
    g_recv,
    g_send,
):
    g = lax.axis_index("groups")
    z = lax.axis_index("col")
    x = lax.axis_index("row")
    s = lax.axis_index("side")
    peer = 1 - s
    gc = nz // nx
    per_group = HEADS // KV_HEADS
    rows = hid_any.shape[0]
    total = nz * rows
    kh = hid_any.shape[1] // 2
    in_half = wq.shape[1]
    out_half = wo.shape[1]
    head_cols = per_group * HEAD_DIM

    def z_at(step):
        return lax.rem(z + step, nz)

    def x_at(step):
        return lax.rem(x + step, nx)

    def remote(src, dst, send, recv, zz, xx, ss):
        return pltpu.make_async_remote_copy(
            src_ref=src,
            dst_ref=dst,
            send_sem=send,
            recv_sem=recv,
            device_id=(g, zz, xx, ss),
            device_id_type=MESH,
        )

    def arrived(ref, sem):
        pltpu.make_async_copy(ref, ref, sem).wait()

    own_x = [
        pltpu.make_async_copy(
            hid_any.at[:, pl.ds(pl.multiple_of(side * kh, 128), kh)], xg.at[side, z], x_recv.at[side, z]
        )
        for side in range(2)
    ]
    for copy in own_x:
        copy.start()

    barrier = pltpu.get_barrier_semaphore()
    greeted = 0
    for step in range(1, nz):
        pl.semaphore_signal(barrier, inc=1, device_id=(g, z_at(step), x, s), device_id_type=MESH)
        greeted += 1
    for step in range(1, nx):
        for side in range(2):
            pl.semaphore_signal(
                barrier, inc=1, device_id=(g, z, x_at(step), side), device_id_type=MESH
            )
            greeted += 1
    pl.semaphore_signal(barrier, inc=1, device_id=(g, z, x, peer), device_id_type=MESH)
    greeted += 1
    pl.semaphore_wait(barrier, greeted)

    waits = []
    for step in range(1, nz):
        copy = remote(
            hid_any.at[:, pl.ds(pl.multiple_of(s * kh, 128), kh)],
            xg.at[s, z],
            x_send.at[step],
            x_recv.at[s, z],
            z_at(step),
            x,
            s,
        )
        copy.start()
        waits.append(copy)

    loads = [
        pltpu.make_async_copy(
            wq_any.at[pl.ds(pl.multiple_of(part * kh, 16), kh), pl.ds(pl.multiple_of(s * in_half, 128), in_half)],
            wq.at[pl.ds(pl.multiple_of(part * kh, 16), kh), :],
            load_sem.at[slot],
        )
        for slot, part in enumerate((s, peer))
    ]
    for j in range(gc):
        lanes = pl.ds(pl.multiple_of((2 * j + s) * HEAD_DIM, 128), HEAD_DIM)
        loads.append(pltpu.make_async_copy(k_any.at[:, :, lanes], kbuf.at[j], load_sem.at[2 + 2 * j]))
        loads.append(pltpu.make_async_copy(v_any.at[:, :, lanes], vbuf.at[j], load_sem.at[3 + 2 * j]))
    loads.append(
        pltpu.make_async_copy(
            wo_any.at[:, pl.ds(pl.multiple_of(s * out_half, 128), out_half)], wo, load_sem.at[2 + 2 * gc]
        )
    )
    loads.append(pltpu.make_async_copy(hid_any, hid, load_sem.at[3 + 2 * gc]))
    for copy in loads:
        copy.start()

    def prepare(side, first):
        for step in range(nz):
            zz = z_at(step)
            arrived(xg.at[side, zz], x_recv.at[side, zz])
            if first and step > 0:
                copy = remote(
                    xg.at[side, zz],
                    xg.at[side, zz],
                    x_fwd.at[step],
                    x_recv.at[side, zz],
                    z,
                    x,
                    peer,
                )
                copy.start()
                waits.append(copy)
            value = xg[side, zz].astype(F32)
            squares = jnp.sum(value * value, axis=1, keepdims=True)
            spread = jnp.broadcast_to(squares, (rows, 128))
            if first:
                sso[zz] = spread
            else:
                sso[zz] = sso[zz] + spread
            xn[side, zz] = (value * gain_ref[side]).astype(BF16)

    def project_in(side, first):
        @pl.loop(0, in_half // TILE)
        def _(n):
            cols = pl.ds(pl.multiple_of(n * TILE, TILE), TILE)
            part = jnp.dot(
                xn[side].reshape(total, kh),
                wq[pl.ds(pl.multiple_of(side * kh, 16), kh), cols],
                preferred_element_type=F32,
            )
            if first:
                acc[:, cols] = part
            else:
                acc[:, cols] = acc[:, cols] + part

    prepare(s, True)
    loads[0].wait()
    project_in(s, True)
    prepare(peer, False)
    ss_waits = []
    for step in range(1, nx):
        copy = remote(sso, ssb.at[x], ss_send.at[step], ss_recv.at[x], z, x_at(step), s)
        copy.start()
        waits.append(copy)
    loads[1].wait()
    project_in(peer, False)
    squares = sso[...]
    for step in range(1, nx):
        xx = x_at(step)
        arrived(ssb.at[xx], ss_recv.at[xx])
        squares = squares + ssb[xx]
    scale = lax.rsqrt(squares.reshape(total, 128) / (2 * kh * nx) + EPSILON)
    scale = jnp.concatenate([scale] * (TILE // 128), axis=1)
    for n in range(in_half // TILE):
        cols = slice(n * TILE, (n + 1) * TILE)
        part = (acc[:, cols] * scale).astype(BF16)
        moved = jnp.dot(to_slot_ref[...], part, preferred_element_type=F32).astype(BF16)
        pbuf[:, :, cols] = moved.reshape(nz, rows, TILE)

    for step in range(1, nz):
        zz = z_at(step)
        copy = remote(pbuf.at[zz], rbuf.at[z], p_send.at[step], p_recv.at[z], zz, x, s)
        copy.start()
        waits.append(copy)
    own_p = pltpu.make_async_copy(pbuf.at[z], rbuf.at[z], p_recv.at[z])
    own_p.start()

    for step in range(1, nx):
        xx = x_at(step)
        for j in range(gc):
            source = xx * gc + j
            arrived(rbuf.at[source], p_recv.at[source])
            copy = remote(
                rbuf.at[source], fbuf.at[x, j], f_send.at[step, j], f_recv.at[x, j], z, xx, s
            )
            copy.start()
            waits.append(copy)

    factor = HEAD_DIM ** (-0.5)
    cache = k_any.shape[1]
    unit = 8
    stack = unit * per_group
    width = unit * cache
    row_id = lax.broadcasted_iota(jnp.int32, (stack, width), 0)
    col_id = lax.broadcasted_iota(jnp.int32, (stack, width), 1)
    diagonal = (row_id % unit) == (col_id // cache)
    position = col_id % cache

    def tall(value):
        return jnp.concatenate([value] * per_group, axis=0)

    def turned(value, cos_vals, sin_vals):
        return (value * cos_vals + pltpu.roll(value, HEAD_DIM // 2, 1) * sin_vals).astype(BF16)

    for j in range(gc):
        source = x * gc + j
        arrived(rbuf.at[source], p_recv.at[source])
        value = rbuf[source].astype(F32)
        for step in range(1, nx):
            xx = x_at(step)
            arrived(fbuf.at[xx, j], f_recv.at[xx, j])
            value = value + fbuf[xx, j].astype(F32)
        tb[...] = value.astype(BF16).astype(F32)
        loads[2 + 2 * j].wait()
        loads[3 + 2 * j].wait()
        for it in range(rows // unit):
            block = slice(it * unit, (it + 1) * unit)
            cos_vals, sin_vals = cos_ref[block, :], sin_ref[block, :]
            heads = jnp.concatenate(
                [tb[block, h * HEAD_DIM : (h + 1) * HEAD_DIM] for h in range(per_group)], axis=0
            )
            queries = turned(heads, tall(cos_vals), tall(sin_vals))
            new_key = turned(
                tb[block, head_cols : head_cols + HEAD_DIM], cos_vals, sin_vals
            ).astype(F32)
            new_value = tb[block, head_cols + HEAD_DIM : head_cols + 2 * HEAD_DIM]
            keys = kbuf[j, block].reshape(width, HEAD_DIM)
            values = vbuf[j, block].reshape(width, HEAD_DIM)
            scores = (
                lax.dot_general(
                    queries, keys, (((1,), (1,)), ((), ())), preferred_element_type=F32
                )
                * factor
            )
            own = jnp.sum(queries.astype(F32) * tall(new_key), axis=1, keepdims=True) * factor
            filled = tall(len_ref[block, :])[:, :1]
            scores = jnp.where(diagonal & (position < filled), scores, -1e30)
            top = jnp.maximum(jnp.max(scores, axis=1, keepdims=True), own)
            weights = jnp.exp(scores - top)
            own_weight = jnp.exp(own - top)
            denominator = jnp.sum(weights, axis=1, keepdims=True) + own_weight
            probs = (weights / denominator).astype(BF16)
            own_prob = (own_weight / denominator).astype(BF16).astype(F32)
            mixed = jnp.dot(probs, values, preferred_element_type=F32) + own_prob * tall(new_value)
            for h in range(per_group):
                af[block, h * HEAD_DIM : (h + 1) * HEAD_DIM] = mixed[h * unit : (h + 1) * unit]
        ag[s, j, z] = af[...].astype(BF16)
        targets = [(z_at(step), s) for step in range(1, nz)] + [(z, peer)]
        for n, (zz, side) in enumerate(targets):
            copy = remote(
                ag.at[s, j, z], ag.at[s, j, z], a_send.at[j, n], a_recv.at[s, j, z], zz, x, side
            )
            copy.start()
            waits.append(copy)

    for j in range(gc):
        for step in range(1, nz):
            zz = z_at(step)
            arrived(ag.at[s, j, zz], a_recv.at[s, j, zz])
            copy = remote(
                ag.at[s, j, zz],
                ag.at[s, j, zz],
                a_fwd.at[j, step],
                a_recv.at[s, j, zz],
                z,
                x,
                peer,
            )
            copy.start()
            waits.append(copy)
    loads[2 + 2 * gc].wait()

    def project_out(side, first):
        @pl.loop(0, out_half // TILE)
        def _(n):
            cols = pl.ds(pl.multiple_of(n * TILE, TILE), TILE)
            part = None
            for j in range(gc):
                depth = pl.ds(pl.multiple_of((2 * j + side) * head_cols, 16), head_cols)
                term = jnp.dot(
                    ag[side, j].reshape(total, head_cols), wo[depth, cols], preferred_element_type=F32
                )
                part = term if part is None else part + term
            if first:
                yacc[:, cols] = part
            else:
                part = (yacc[:, cols] + part).astype(BF16)
                moved = jnp.dot(to_req_ref[...], part, preferred_element_type=F32).astype(BF16)
                ybuf[:, :, cols] = moved.reshape(nz, rows, TILE)

    project_out(s, True)
    for j in range(gc):
        for step in range(nz):
            zz = z_at(step)
            arrived(ag.at[peer, j, zz], a_recv.at[peer, j, zz])
    project_out(peer, False)

    for step in range(1, nz):
        zz = z_at(step)
        copy = remote(ybuf.at[zz], hbuf.at[z], y_send.at[step], y_recv.at[z], zz, x, s)
        copy.start()
        waits.append(copy)
    own_y = pltpu.make_async_copy(ybuf.at[z], hbuf.at[z], y_recv.at[z])
    own_y.start()

    for step in range(1, nx):
        xx = x_at(step)
        for j in range(gc):
            source = xx * gc + j
            arrived(hbuf.at[source], y_recv.at[source])
            copy = remote(
                hbuf.at[source],
                gbuf.at[x, s, j],
                g_send.at[step, j],
                g_recv.at[x, s, j],
                z,
                xx,
                0,
            )
            copy.start()
            waits.append(copy)

    loads[3 + 2 * gc].wait()
    for j in range(gc):
        source = x * gc + j
        arrived(hbuf.at[source], y_recv.at[source])

    @pl.when(s == 1)
    def _():
        across = []
        for j in range(gc):
            copy = remote(
                hbuf.at[x * gc + j],
                gbuf.at[x, s, j],
                g_send.at[0, j],
                g_recv.at[x, s, j],
                z,
                x,
                0,
            )
            copy.start()
            across.append(copy)
        for j in range(gc):
            for side in range(2):
                lanes = slice((2 * j + side) * head_cols, (2 * j + side + 1) * head_cols)
                out_ref[0, :, lanes] = ag[side, j, z]
        for copy in across:
            copy.wait_send()

    @pl.when(s == 0)
    def _():
        for j in range(gc):
            for side in range(2):
                lanes = slice((2 * j + side) * out_half, (2 * j + side + 1) * out_half)
                value = hid[:, lanes].astype(F32)
                if side == 0:
                    mine = hbuf[x * gc + j].astype(F32)
                else:
                    arrived(gbuf.at[x, 1, j], g_recv.at[x, 1, j])
                    mine = gbuf[x, 1, j].astype(F32)
                for step in range(1, nx):
                    xx = x_at(step)
                    arrived(gbuf.at[xx, side, j], g_recv.at[xx, side, j])
                    mine = mine + gbuf[xx, side, j].astype(F32)
                out_ref[0, :, lanes] = (value + mine).astype(BF16)

    for copy in waits:
        copy.wait_send()


def per_device_fused(
    hidden_in,
    norm_gain,
    qkv_weight,
    out_weight,
    key_cache,
    value_cache,
    cache_lengths,
    slot_request,
):
    nz = lax.axis_size("col")
    nx = lax.axis_size("row")
    gc = nz // nx
    rows, columns = hidden_in.shape
    slots, cache, _ = key_cache.shape
    kh = columns // 2
    total = nz * rows
    in_half = qkv_weight.shape[1] // 2
    out_half = out_weight.shape[1] // 2
    head_cols = HEADS // KV_HEADS * HEAD_DIM
    cos_vals, sin_vals = rope_tables(cache_lengths, HEAD_DIM)
    cos_full = jnp.concatenate([cos_vals, cos_vals], axis=1)
    sin_full = jnp.concatenate([-sin_vals, sin_vals], axis=1)
    filled = jnp.broadcast_to(cache_lengths[:, None], (slots, 128))
    ids = jnp.arange(total, dtype=jnp.int32)
    to_slot = (slot_request[:, None] == ids[None, :]).astype(BF16)
    to_req = (ids[:, None] == slot_request[None, :]).astype(BF16)
    vmem = pl.BlockSpec(memory_space=pltpu.VMEM)
    far = pl.BlockSpec(memory_space=pl.ANY)
    dma = pltpu.SemaphoreType.DMA
    return pl.pallas_call(
        functools.partial(fused_kernel, nz, nx),
        out_shape=jax.ShapeDtypeStruct((1, rows, columns), BF16),
        in_specs=[far, vmem, far, far, far, far, vmem, vmem, vmem, vmem, vmem],
        out_specs=vmem,
        scratch_shapes=[
            pltpu.VMEM((columns, in_half), BF16),
            pltpu.VMEM((columns, out_half), BF16),
            pltpu.VMEM((gc, slots, cache, HEAD_DIM), BF16),
            pltpu.VMEM((gc, slots, cache, HEAD_DIM), BF16),
            pltpu.VMEM((rows, columns), BF16),
            pltpu.VMEM((2, nz, rows, kh), BF16),
            pltpu.VMEM((2, nz, rows, kh), BF16),
            pltpu.VMEM((nz, rows, 128), F32),
            pltpu.VMEM((nx, nz, rows, 128), F32),
            pltpu.VMEM((total, in_half), F32),
            pltpu.VMEM((nz, rows, in_half), BF16),
            pltpu.VMEM((nz, rows, in_half), BF16),
            pltpu.VMEM((nx, gc, rows, in_half), BF16),
            pltpu.VMEM((rows, in_half), F32),
            pltpu.VMEM((rows, head_cols), F32),
            pltpu.VMEM((2, gc, nz, rows, head_cols), BF16),
            pltpu.VMEM((total, out_half), F32),
            pltpu.VMEM((nz, rows, out_half), BF16),
            pltpu.VMEM((nz, rows, out_half), BF16),
            pltpu.VMEM((nx, 2, gc, rows, out_half), BF16),
            dma((4 + 2 * gc,)),
            dma((2, nz)),
            dma((nz,)),
            dma((nz,)),
            dma((nx,)),
            dma((nx,)),
            dma((nz,)),
            dma((nz,)),
            dma((nx, gc)),
            dma((nx, gc)),
            dma((2, gc, nz)),
            dma((gc, nz)),
            dma((gc, nz)),
            dma((nz,)),
            dma((nz,)),
            dma((nx, 2, gc)),
            dma((nx, gc)),
        ],
        compiler_params=pltpu.CompilerParams(
            collective_id=0, has_side_effects=True, vmem_limit_bytes=60 * 1024 * 1024
        ),
    )(
        hidden_in,
        norm_gain.reshape(2, 1, kh),
        qkv_weight,
        out_weight,
        key_cache,
        value_cache,
        cos_full,
        sin_full,
        filled,
        to_slot,
        to_req,
    )


def per_device(
    hidden_in,
    norm_gain,
    qkv_weight,
    out_weight,
    key_cache,
    value_cache,
    cache_lengths,
    slot_request,
):
    group_width = (HEADS // KV_HEADS + 2) * HEAD_DIM
    aligned = (
        qkv_weight.shape[1] == 2 * group_width
        and out_weight.shape[1] % (2 * TILE) == 0
        and lax.axis_size("col") % lax.axis_size("row") == 0
        and hidden_in.shape[0] % 16 == 0
        and hidden_in.shape[1] % 256 == 0
        and key_cache.shape[0] == hidden_in.shape[0]
    )
    body = per_device_fused if aligned else per_device_general
    return body(
        hidden_in,
        norm_gain,
        qkv_weight,
        out_weight,
        key_cache,
        value_cache,
        cache_lengths,
        slot_request,
    )


def solution(mesh):
    placed = (
        P(("groups", "col"), "row"),
        P("row"),
        P("row", "col"),
        P("row", "col"),
        P(("groups", "col"), None, "row"),
        P(("groups", "col"), None, "row"),
        P(("groups", "col")),
        P("groups"),
    )
    return jax.shard_map(
        per_device,
        mesh=mesh,
        in_specs=placed,
        out_specs=P("side", ("groups", "col"), "row"),
        check_vma=False,
    )
```

```python
import functools

import jax
import jax.numpy as jnp
from jax import lax
from jax.experimental import pallas as pl
from jax.experimental.pallas import tpu as pltpu
from jax.sharding import PartitionSpec as P

D = 8192
HEADS = 64
KV_HEADS = 8
HEAD_DIM = 128
QKV = 10240


EPSILON = 1e-05
THETA = 500000.0


def swapped(value, axis, bit):
    mask = 2**bit
    pairs = [(source, source ^ mask) for source in range(lax.axis_size(axis))]
    return lax.ppermute(value, axis, pairs)


def rope_tables(lengths, head_dim):
    half_dim = head_dim // 2
    inv_freq = jnp.exp(
        -jnp.log(jnp.float32(THETA)) * jnp.arange(half_dim, dtype=jnp.float32) / half_dim
    )
    phases = lengths.astype(jnp.float32)[:, None] * inv_freq[None, :]
    return (jnp.cos(phases), jnp.sin(phases))


def rotate(vector, cos_vals, sine_vals):
    half_dim = vector.shape[-1] // 2
    front_half = vector[..., :half_dim]
    back_half = vector[..., half_dim:]
    return jnp.concatenate(
        [
            front_half * cos_vals - back_half * sine_vals,
            back_half * cos_vals + front_half * sine_vals,
        ],
        axis=-1,
    )


def attend(packed, key_block, value_block, lengths):
    slot_count = packed.shape[0]
    cache_size = key_block.shape[1]
    groups = key_block.shape[2] // HEAD_DIM
    per_group = HEADS // KV_HEADS
    grouped = packed.reshape(slot_count, groups, per_group + 2, HEAD_DIM)
    cos_vals, sine_vals = rope_tables(lengths, HEAD_DIM)
    queries = rotate(
        grouped[:, :, :per_group].astype(jnp.float32),
        cos_vals[:, None, None, :],
        sine_vals[:, None, None, :],
    ).astype(jnp.bfloat16)
    new_keys = rotate(
        grouped[:, :, per_group].astype(jnp.float32), cos_vals[:, None, :], sine_vals[:, None, :]
    ).astype(jnp.bfloat16)
    new_values = grouped[:, :, per_group + 1]
    cache_keys = key_block.reshape(slot_count, cache_size, groups, HEAD_DIM)
    cache_values = value_block.reshape(slot_count, cache_size, groups, HEAD_DIM)
    factor = HEAD_DIM ** (-0.5)
    cache_scores = (
        jnp.einsum("sghd,slgd->sghl", queries, cache_keys, preferred_element_type=jnp.float32)
        * factor
    )
    own_scores = (
        jnp.einsum("sghd,sgd->sgh", queries, new_keys, preferred_element_type=jnp.float32) * factor
    )
    in_cache = lax.broadcasted_iota(jnp.int32, (slot_count, cache_size), 1) < lengths[:, None]
    cache_scores = jnp.where(in_cache[:, None, None, :], cache_scores, -1e30)
    row_max = jnp.maximum(jnp.max(cache_scores, axis=-1), own_scores)
    cache_exp = jnp.exp(cache_scores - row_max[..., None])
    own_exp = jnp.exp(own_scores - row_max)
    denominator = jnp.sum(cache_exp, axis=-1) + own_exp
    cache_weight = (cache_exp / denominator[..., None]).astype(jnp.bfloat16)
    own_weight = (own_exp / denominator).astype(jnp.bfloat16)
    combined = jnp.einsum(
        "sghl,slgd->sghd", cache_weight, cache_values, preferred_element_type=jnp.float32
    )
    combined = (
        combined
        + own_weight.astype(jnp.float32)[..., None] * new_values.astype(jnp.float32)[:, :, None, :]
    )
    return combined.astype(jnp.bfloat16).reshape(slot_count, groups * per_group * HEAD_DIM)


def per_device_general(
    hidden_in,
    norm_gain,
    qkv_weight,
    out_weight,
    key_cache,
    value_cache,
    cache_lengths,
    slot_request,
):
    side_index = lax.axis_index("side")
    is_weight = side_index == 0
    col_count = lax.axis_size("col")
    row_count = lax.axis_size("row")
    group_cols = col_count // row_count
    in_half = qkv_weight.shape[1] // 2
    out_half = out_weight.shape[1] // 2
    residual = hidden_in.astype(jnp.float32)
    square_sums = lax.psum(jnp.sum(residual * residual, axis=1), "row")
    normed = (
        residual
        * lax.rsqrt(square_sums[:, None] / D + EPSILON)
        * norm_gain.astype(jnp.float32)[None, :]
    ).astype(jnp.bfloat16)
    in_weight = lax.dynamic_slice_in_dim(qkv_weight, side_index * in_half, in_half, 1)
    partial_in = jnp.dot(
        lax.all_gather(normed, "col", axis=0, tiled=True),
        in_weight,
        preferred_element_type=jnp.float32,
    )
    in_slots = jnp.take(partial_in, slot_request, axis=0)
    own_width = QKV // row_count
    summed = lax.psum(in_slots.astype(jnp.bfloat16), "row")
    spread = lax.all_to_all(summed, "col", split_axis=0, concat_axis=1, tiled=True)
    own_columns = lax.dynamic_slice_in_dim(
        spread.reshape(spread.shape[0], col_count, in_half),
        lax.axis_index("row") * group_cols,
        group_cols,
        1,
    )
    slot_half = key_cache.shape[0] // 2
    halves = lax.all_to_all(
        own_columns[:, :, None, :], "side", split_axis=0, concat_axis=2, tiled=True
    )
    arrived = halves.reshape(slot_half, own_width)
    first_slot = side_index * slot_half
    key_part = lax.dynamic_slice_in_dim(key_cache, first_slot, slot_half, 0)
    value_part = lax.dynamic_slice_in_dim(value_cache, first_slot, slot_half, 0)
    length_part = lax.dynamic_slice_in_dim(cache_lengths, first_slot, slot_half, 0)
    attended = attend(arrived, key_part, value_part, length_part)
    out_cols = lax.dynamic_slice_in_dim(out_weight, side_index * out_half, out_half, 1)
    collected = lax.all_gather(attended, ("col", "side"), axis=0, tiled=True)
    out_slots = jnp.dot(collected, out_cols, preferred_element_type=jnp.float32)
    inverse = jnp.argsort(slot_request)
    out_requests = jnp.take(out_slots, inverse, axis=0)
    spread_out = lax.all_to_all(
        out_requests.astype(jnp.bfloat16), "col", split_axis=0, concat_axis=1, tiled=True
    ).astype(out_requests.dtype)
    out_view = spread_out.reshape(spread_out.shape[0], col_count, out_half)
    summed_out = lax.psum_scatter(
        out_view.astype(jnp.bfloat16), "row", scatter_dimension=1, tiled=True
    ).astype(jnp.float32)
    req_rows = hidden_in.shape[0]
    residual_view = residual.reshape(req_rows, group_cols, 2, out_half)
    residual_half = lax.dynamic_index_in_dim(residual_view, side_index, 2, keepdims=False)
    own_hidden = (residual_half + summed_out).astype(jnp.bfloat16)
    payload = jnp.where(is_weight, attended, own_hidden.reshape(attended.shape))
    received = swapped(payload, "side", 0)
    hidden = jnp.stack([own_hidden, received.reshape(own_hidden.shape)], axis=2).reshape(
        req_rows, residual.shape[1]
    )
    attention_rows = jnp.concatenate([received, attended], axis=0)
    result = jnp.where(is_weight, hidden, attention_rows)
    return result[None]


MESH = pl.DeviceIdType.MESH
F32 = jnp.float32
BF16 = jnp.bfloat16
TILE = 256


def fused_kernel(
    nz,
    nx,
    hid_any,
    gain_any,
    wq_any,
    wo_any,
    k_any,
    v_any,
    len_any,
    req_any,
    out_any,
    wq,
    wo,
    kbuf,
    vbuf,
    hid,
    xg,
    xn,
    sso,
    ssb,
    acc,
    pbuf,
    rbuf,
    fbuf,
    tb,
    af,
    ag,
    yacc,
    ybuf,
    hbuf,
    gbuf,
    gain_buf,
    len_buf,
    req_buf,
    cos_ref,
    sin_ref,
    len_ref,
    to_slot_ref,
    to_req_ref,
    scale_buf,
    out_ref,
    small_sem,
    load_sem,
    x_recv,
    x_send,
    x_fwd,
    ss_recv,
    ss_send,
    p_recv,
    p_send,
    f_recv,
    f_send,
    a_recv,
    a_send,
    a_fwd,
    y_recv,
    y_send,
    g_recv,
    g_send,
):
    g = lax.axis_index("groups")
    z = lax.axis_index("col")
    x = lax.axis_index("row")
    s = lax.axis_index("side")
    peer = 1 - s
    gc = nz // nx
    per_group = HEADS // KV_HEADS
    rows = hid_any.shape[0]
    total = nz * rows
    kh = hid_any.shape[1] // 2
    in_half = wq.shape[1]
    out_half = wo.shape[1]
    head_cols = per_group * HEAD_DIM

    def z_at(step):
        return lax.rem(z + step, nz)

    def x_at(step):
        return lax.rem(x + step, nx)

    def remote(src, dst, send, recv, zz, xx, ss):
        return pltpu.make_async_remote_copy(
            src_ref=src,
            dst_ref=dst,
            send_sem=send,
            recv_sem=recv,
            device_id=(g, zz, xx, ss),
            device_id_type=MESH,
        )

    def arrived(ref, sem):
        pltpu.make_async_copy(ref, ref, sem).wait()

    own_x = [
        pltpu.make_async_copy(
            hid_any.at[:, pl.ds(pl.multiple_of(side * kh, 128), kh)], xg.at[side, z], x_recv.at[side, z]
        )
        for side in range(2)
    ]
    small = [
        pltpu.make_async_copy(far, near, small_sem.at[slot])
        for slot, (far, near) in enumerate(
            ((gain_any, gain_buf), (len_any, len_buf), (req_any, req_buf))
        )
    ]
    for copy in own_x + small:
        copy.start()

    hid_load = pltpu.make_async_copy(hid_any, hid, load_sem.at[3 + 2 * gc])
    hid_load.start()

    barrier = pltpu.get_barrier_semaphore()
    greeted = 0
    for step in range(1, nz):
        pl.semaphore_signal(barrier, inc=1, device_id=(g, z_at(step), x, s), device_id_type=MESH)
        greeted += 1
    for step in range(1, nx):
        for side in range(2):
            pl.semaphore_signal(
                barrier, inc=1, device_id=(g, z, x_at(step), side), device_id_type=MESH
            )
            greeted += 1
    pl.semaphore_signal(barrier, inc=1, device_id=(g, z, x, peer), device_id_type=MESH)
    greeted += 1
    hid_load.wait()
    pl.semaphore_wait(barrier, greeted)

    waits = []
    for step in range(1, nz):
        copy = remote(
            hid.at[:, pl.ds(pl.multiple_of(s * kh, 128), kh)],
            xg.at[s, z],
            x_send.at[step],
            x_recv.at[s, z],
            z_at(step),
            x,
            s,
        )
        copy.start()
        waits.append(copy)

    loads = [
        pltpu.make_async_copy(
            wq_any.at[pl.ds(pl.multiple_of(part * kh, 16), kh), pl.ds(pl.multiple_of(s * in_half, 128), in_half)],
            wq.at[pl.ds(pl.multiple_of(part * kh, 16), kh), :],
            load_sem.at[slot],
        )
        for slot, part in enumerate((s, peer))
    ]
    for j in range(gc):
        lanes = pl.ds(pl.multiple_of((2 * j + s) * HEAD_DIM, 128), HEAD_DIM)
        loads.append(pltpu.make_async_copy(k_any.at[:, :, lanes], kbuf.at[j], load_sem.at[2 + 2 * j]))
        loads.append(pltpu.make_async_copy(v_any.at[:, :, lanes], vbuf.at[j], load_sem.at[3 + 2 * j]))
    loads.append(
        pltpu.make_async_copy(
            wo_any.at[:, pl.ds(pl.multiple_of(s * out_half, 128), out_half)], wo, load_sem.at[2 + 2 * gc]
        )
    )
    for copy in loads:
        copy.start()

    for copy in small:
        copy.wait()
    wide = (total, total)
    owner = jnp.broadcast_to(req_buf[...].reshape(1, total), wide)
    to_req = (owner == lax.broadcasted_iota(jnp.int32, wide, 0)).astype(F32)
    to_req_ref[...] = to_req.astype(BF16)
    to_slot_ref[...] = to_req.T.astype(BF16)
    slots = k_any.shape[0]
    square = (slots, slots)
    across = jnp.broadcast_to(len_buf[...].reshape(1, slots), square).astype(F32)
    on_diagonal = lax.broadcasted_iota(jnp.int32, square, 0) == lax.broadcasted_iota(
        jnp.int32, square, 1
    )
    lengths = jnp.sum(jnp.where(on_diagonal, across, 0.0), axis=1, keepdims=True)
    lengths = jnp.broadcast_to(lengths, (slots, HEAD_DIM))
    len_ref[...] = lengths
    half_dim = HEAD_DIM // 2
    lane = lax.broadcasted_iota(jnp.int32, (slots, HEAD_DIM), 1)
    exponent = lax.rem(lane, half_dim).astype(F32)
    phases = lengths * jnp.exp(-jnp.log(jnp.full((1, 1), THETA, F32)) * exponent / half_dim)
    cos_ref[...] = jnp.cos(phases)
    sin_ref[...] = jnp.where(lane < half_dim, -1.0, 1.0) * jnp.sin(phases)

    def prepare(side, first):
        gain = gain_buf[pl.ds(pl.multiple_of(side * kh, 128), kh)].astype(F32).reshape(1, kh)
        for step in range(nz):
            zz = z_at(step)
            arrived(xg.at[side, zz], x_recv.at[side, zz])
            if first and step > 0:
                copy = remote(
                    xg.at[side, zz],
                    xg.at[side, zz],
                    x_fwd.at[step],
                    x_recv.at[side, zz],
                    z,
                    x,
                    peer,
                )
                copy.start()
                waits.append(copy)
            value = xg[side, zz].astype(F32)
            squares = jnp.sum(value * value, axis=1, keepdims=True)
            spread = jnp.broadcast_to(squares, (rows, 128))
            if first:
                sso[zz] = spread
            else:
                sso[zz] = sso[zz] + spread
            xn[side, zz] = (value * gain).astype(BF16)

    def project_in(side):
        @pl.loop(0, in_half // TILE)
        def _(n):
            cols = pl.ds(pl.multiple_of(n * TILE, TILE), TILE)
            acc[:, cols] = jnp.dot(
                xn[side].reshape(total, kh),
                wq[pl.ds(pl.multiple_of(side * kh, 16), kh), cols],
                preferred_element_type=F32,
            )

    prepare(s, True)
    loads[0].wait()
    project_in(s)
    prepare(peer, False)
    for step in range(1, nx):
        copy = remote(sso, ssb.at[x], ss_send.at[step], ss_recv.at[x], z, x_at(step), s)
        copy.start()
        waits.append(copy)
    loads[1].wait()
    in_chunks = in_half // TILE
    for n in range(in_chunks):
        cols = slice(n * TILE, (n + 1) * TILE)
        part = acc[:, cols] + jnp.dot(
            xn[peer].reshape(total, kh),
            wq[pl.ds(pl.multiple_of(peer * kh, 16), kh), cols],
            preferred_element_type=F32,
        )
        moved = jnp.dot(to_slot_ref[...], part.astype(BF16), preferred_element_type=F32)
        pbuf[n] = moved.astype(BF16).reshape(nz, rows, TILE)
        for step in range(1, nz):
            zz = z_at(step)
            copy = remote(
                pbuf.at[n, zz], rbuf.at[n, z], p_send.at[step, n], p_recv.at[z, n], zz, x, s
            )
            copy.start()
            waits.append(copy)
        pltpu.make_async_copy(pbuf.at[n, z], rbuf.at[n, z], p_recv.at[z, n]).start()

    squares = sso[...]
    for step in range(1, nx):
        xx = x_at(step)
        arrived(ssb.at[xx], ss_recv.at[xx])
        squares = squares + ssb[xx]
    flat = jnp.broadcast_to(squares.reshape(total, 128).T[:1, :], (total, total))
    by_slot = jnp.sum(to_slot_ref[...].astype(F32) * flat, axis=1, keepdims=True)
    scale = lax.rsqrt(by_slot / (2 * kh * nx) + EPSILON)
    scale_buf[...] = jnp.broadcast_to(scale, (total, 128)).reshape(nz, rows, 128)

    for n in range(in_chunks):
        for j in range(gc):
            for step in range(1, nx):
                xx = x_at(step)
                source = xx * gc + j
                arrived(rbuf.at[n, source], p_recv.at[source, n])
                copy = remote(
                    rbuf.at[n, source],
                    fbuf.at[x, j, n],
                    f_send.at[step, j, n],
                    f_recv.at[x, j, n],
                    z,
                    xx,
                    s,
                )
                copy.start()
                waits.append(copy)

    factor = HEAD_DIM ** (-0.5)
    cache = k_any.shape[1]
    unit = 8
    stack = unit * per_group
    width = unit * cache
    row_id = lax.broadcasted_iota(jnp.int32, (stack, width), 0)
    col_id = lax.broadcasted_iota(jnp.int32, (stack, width), 1)
    diagonal = (row_id % unit) == (col_id // cache)
    position = (col_id % cache).astype(F32)

    def tall(value):
        return jnp.concatenate([value] * per_group, axis=0)

    def turned(value, cos_vals, sin_vals):
        return (value * cos_vals + pltpu.roll(value, HEAD_DIM // 2, 1) * sin_vals).astype(BF16)

    for j in range(gc):
        source = x * gc + j
        own_scale = scale_buf[z][:, :1]
        for n in range(in_chunks):
            arrived(rbuf.at[n, source], p_recv.at[source, n])
            value = rbuf[n, source].astype(F32)
            for step in range(1, nx):
                xx = x_at(step)
                arrived(fbuf.at[xx, j, n], f_recv.at[xx, j, n])
                value = value + fbuf[xx, j, n].astype(F32)
            tb[:, n * TILE : (n + 1) * TILE] = (value * own_scale).astype(BF16).astype(F32)
        loads[2 + 2 * j].wait()
        loads[3 + 2 * j].wait()
        for it in range(rows // unit):
            block = slice(it * unit, (it + 1) * unit)
            cos_vals, sin_vals = cos_ref[block, :], sin_ref[block, :]
            heads = jnp.concatenate(
                [tb[block, h * HEAD_DIM : (h + 1) * HEAD_DIM] for h in range(per_group)], axis=0
            )
            queries = turned(heads, tall(cos_vals), tall(sin_vals))
            new_key = turned(
                tb[block, head_cols : head_cols + HEAD_DIM], cos_vals, sin_vals
            ).astype(F32)
            new_value = tb[block, head_cols + HEAD_DIM : head_cols + 2 * HEAD_DIM]
            keys = kbuf[j, block].reshape(width, HEAD_DIM)
            values = vbuf[j, block].reshape(width, HEAD_DIM)
            scores = (
                lax.dot_general(
                    queries, keys, (((1,), (1,)), ((), ())), preferred_element_type=F32
                )
                * factor
            )
            own = jnp.sum(queries.astype(F32) * tall(new_key), axis=1, keepdims=True) * factor
            filled = tall(len_ref[block, :])[:, :1]
            scores = jnp.where(diagonal & (position < filled), scores, -1e30)
            top = jnp.maximum(jnp.max(scores, axis=1, keepdims=True), own)
            weights = jnp.exp(scores - top)
            own_weight = jnp.exp(own - top)
            denominator = jnp.sum(weights, axis=1, keepdims=True) + own_weight
            probs = (weights / denominator).astype(BF16)
            own_prob = (own_weight / denominator).astype(BF16).astype(F32)
            mixed = jnp.dot(probs, values, preferred_element_type=F32) + own_prob * tall(new_value)
            for h in range(per_group):
                af[block, h * HEAD_DIM : (h + 1) * HEAD_DIM] = mixed[h * unit : (h + 1) * unit]
        ag[s, j, z] = af[...].astype(BF16)
        targets = [(z_at(step), s) for step in range(1, nz)] + [(z, peer)]
        for n, (zz, side) in enumerate(targets):
            copy = remote(
                ag.at[s, j, z], ag.at[s, j, z], a_send.at[j, n], a_recv.at[s, j, z], zz, x, side
            )
            copy.start()
            waits.append(copy)

    for j in range(gc):
        for step in range(1, nz):
            zz = z_at(step)
            arrived(ag.at[s, j, zz], a_recv.at[s, j, zz])
            copy = remote(
                ag.at[s, j, zz],
                ag.at[s, j, zz],
                a_fwd.at[j, step],
                a_recv.at[s, j, zz],
                z,
                x,
                peer,
            )
            copy.start()
            waits.append(copy)
    loads[2 + 2 * gc].wait()

    def out_part(side, cols):
        part = None
        for j in range(gc):
            depth = pl.ds(pl.multiple_of((2 * j + side) * head_cols, 16), head_cols)
            term = jnp.dot(
                ag[side, j].reshape(total, head_cols), wo[depth, cols], preferred_element_type=F32
            )
            part = term if part is None else part + term
        return part

    @pl.loop(0, out_half // TILE)
    def _(n):
        cols = pl.ds(pl.multiple_of(n * TILE, TILE), TILE)
        yacc[:, cols] = out_part(s, cols)

    for j in range(gc):
        for step in range(nz):
            zz = z_at(step)
            arrived(ag.at[peer, j, zz], a_recv.at[peer, j, zz])
    out_chunks = out_half // TILE
    for n in range(out_chunks):
        cols = slice(n * TILE, (n + 1) * TILE)
        part = (yacc[:, cols] + out_part(peer, cols)).astype(BF16)
        moved = jnp.dot(to_req_ref[...], part, preferred_element_type=F32)
        ybuf[n] = moved.astype(BF16).reshape(nz, rows, TILE)
        for step in range(1, nz):
            zz = z_at(step)
            copy = remote(
                ybuf.at[n, zz], hbuf.at[n, z], y_send.at[step, n], y_recv.at[z, n], zz, x, s
            )
            copy.start()
            waits.append(copy)
        pltpu.make_async_copy(ybuf.at[n, z], hbuf.at[n, z], y_recv.at[z, n]).start()

    for n in range(out_chunks):
        for j in range(gc):
            for step in range(1, nx):
                xx = x_at(step)
                source = xx * gc + j
                arrived(hbuf.at[n, source], y_recv.at[source, n])
                copy = remote(
                    hbuf.at[n, source],
                    gbuf.at[x, s, j, n],
                    g_send.at[step, j, n],
                    g_recv.at[x, s, j, n],
                    z,
                    xx,
                    0,
                )
                copy.start()
                waits.append(copy)

    @pl.when(s == 1)
    def _():
        across = []
        for n in range(out_chunks):
            for j in range(gc):
                source = x * gc + j
                arrived(hbuf.at[n, source], y_recv.at[source, n])
                copy = remote(
                    hbuf.at[n, source],
                    gbuf.at[x, s, j, n],
                    g_send.at[0, j, n],
                    g_recv.at[x, s, j, n],
                    z,
                    x,
                    0,
                )
                copy.start()
                across.append(copy)
        for j in range(gc):
            for side in range(2):
                lanes = slice((2 * j + side) * head_cols, (2 * j + side + 1) * head_cols)
                out_ref[0, :, lanes] = ag[side, j, z]
        for copy in across:
            copy.wait_send()

    @pl.when(s == 0)
    def _():
        for n in range(out_chunks):
            for j in range(gc):
                source = x * gc + j
                for side in range(2):
                    begin = (2 * j + side) * out_half + n * TILE
                    lanes = slice(begin, begin + TILE)
                    value = hid[:, lanes].astype(F32)
                    if side == 0:
                        arrived(hbuf.at[n, source], y_recv.at[source, n])
                        mine = hbuf[n, source].astype(F32)
                    else:
                        arrived(gbuf.at[x, 1, j, n], g_recv.at[x, 1, j, n])
                        mine = gbuf[x, 1, j, n].astype(F32)
                    for step in range(1, nx):
                        xx = x_at(step)
                        arrived(gbuf.at[xx, side, j, n], g_recv.at[xx, side, j, n])
                        mine = mine + gbuf[xx, side, j, n].astype(F32)
                    out_ref[0, :, lanes] = (value + mine).astype(BF16)

    written = pltpu.make_async_copy(out_ref, out_any, small_sem.at[3])
    written.start()
    for copy in waits:
        copy.wait_send()
    written.wait()


def per_device_fused(
    hidden_in,
    norm_gain,
    qkv_weight,
    out_weight,
    key_cache,
    value_cache,
    cache_lengths,
    slot_request,
):
    nz = lax.axis_size("col")
    nx = lax.axis_size("row")
    gc = nz // nx
    rows, columns = hidden_in.shape
    slots, cache, _ = key_cache.shape
    kh = columns // 2
    total = nz * rows
    in_half = qkv_weight.shape[1] // 2
    out_half = out_weight.shape[1] // 2
    head_cols = HEADS // KV_HEADS * HEAD_DIM
    nc, ny = in_half // TILE, out_half // TILE
    far = pl.BlockSpec(memory_space=pl.ANY)
    dma = pltpu.SemaphoreType.DMA
    return pl.pallas_call(
        functools.partial(fused_kernel, nz, nx),
        out_shape=jax.ShapeDtypeStruct((1, rows, columns), BF16),
        in_specs=[pl.BlockSpec(memory_space=pltpu.HBM)] * 8,
        out_specs=far,
        scratch_shapes=[
            pltpu.VMEM((columns, in_half), BF16),
            pltpu.VMEM((columns, out_half), BF16),
            pltpu.VMEM((gc, slots, cache, HEAD_DIM), BF16),
            pltpu.VMEM((gc, slots, cache, HEAD_DIM), BF16),
            pltpu.VMEM((rows, columns), BF16),
            pltpu.VMEM((2, nz, rows, kh), BF16),
            pltpu.VMEM((2, nz, rows, kh), BF16),
            pltpu.VMEM((nz, rows, 128), F32),
            pltpu.VMEM((nx, nz, rows, 128), F32),
            pltpu.VMEM((total, in_half), F32),
            pltpu.VMEM((nc, nz, rows, TILE), BF16),
            pltpu.VMEM((nc, nz, rows, TILE), BF16),
            pltpu.VMEM((nx, gc, nc, rows, TILE), BF16),
            pltpu.VMEM((rows, in_half), F32),
            pltpu.VMEM((rows, head_cols), F32),
            pltpu.VMEM((2, gc, nz, rows, head_cols), BF16),
            pltpu.VMEM((total, out_half), F32),
            pltpu.VMEM((ny, nz, rows, TILE), BF16),
            pltpu.VMEM((ny, nz, rows, TILE), BF16),
            pltpu.VMEM((nx, 2, gc, ny, rows, TILE), BF16),
            pltpu.VMEM((columns,), BF16),
            pltpu.VMEM((slots,), jnp.int32),
            pltpu.VMEM((total,), jnp.int32),
            pltpu.VMEM((slots, HEAD_DIM), F32),
            pltpu.VMEM((slots, HEAD_DIM), F32),
            pltpu.VMEM((slots, HEAD_DIM), F32),
            pltpu.VMEM((total, total), BF16),
            pltpu.VMEM((total, total), BF16),
            pltpu.VMEM((nz, rows, 128), F32),
            pltpu.VMEM((1, rows, columns), BF16),
            dma((4,)),
            dma((4 + 2 * gc,)),
            dma((2, nz)),
            dma((nz,)),
            dma((nz,)),
            dma((nx,)),
            dma((nx,)),
            dma((nz, nc)),
            dma((nz, nc)),
            dma((nx, gc, nc)),
            dma((nx, gc, nc)),
            dma((2, gc, nz)),
            dma((gc, nz)),
            dma((gc, nz)),
            dma((nz, ny)),
            dma((nz, ny)),
            dma((nx, 2, gc, ny)),
            dma((nx, gc, ny)),
        ],
        compiler_params=pltpu.CompilerParams(
            collective_id=0, has_side_effects=True, vmem_limit_bytes=60 * 1024 * 1024
        ),
    )(
        hidden_in,
        norm_gain,
        qkv_weight,
        out_weight,
        key_cache,
        value_cache,
        cache_lengths,
        slot_request,
    )


def per_device(
    hidden_in,
    norm_gain,
    qkv_weight,
    out_weight,
    key_cache,
    value_cache,
    cache_lengths,
    slot_request,
):
    group_width = (HEADS // KV_HEADS + 2) * HEAD_DIM
    aligned = (
        qkv_weight.shape[1] == 2 * group_width
        and out_weight.shape[1] % (2 * TILE) == 0
        and lax.axis_size("col") % lax.axis_size("row") == 0
        and hidden_in.shape[0] % 16 == 0
        and hidden_in.shape[1] % 256 == 0
        and key_cache.shape[0] == hidden_in.shape[0]
    )
    body = per_device_fused if aligned else per_device_general
    return body(
        hidden_in,
        norm_gain,
        qkv_weight,
        out_weight,
        key_cache,
        value_cache,
        cache_lengths,
        slot_request,
    )


def solution(mesh):
    placed = (
        P(("groups", "col"), "row"),
        P("row"),
        P("row", "col"),
        P("row", "col"),
        P(("groups", "col"), None, "row"),
        P(("groups", "col"), None, "row"),
        P(("groups", "col")),
        P("groups"),
    )
    return jax.shard_map(
        per_device,
        mesh=mesh,
        in_specs=placed,
        out_specs=P("side", ("groups", "col"), "row"),
        check_vma=False,
    )
```
